512 devices in a mesh: expert: 32 (over z, core), fsdp: 16 (over y, x).
Axes of the slice: x: 4, y: 4, z: 16, core: 2. Of those that a mesh axis runs over, the one named last changes fastest.
Arguments:
- states: bfloat16 [65536, 512], P(('expert', 'fsdp')), may hold values from -6 to 6
- rates: bfloat16 [65536, 512], P(('expert', 'fsdp')), may hold values from -6 to 6
- expert_ids: int32 [65536, 2], P(('expert', 'fsdp')), may hold values from 0 to 63, all different within a row; in each aligned block of 128 rows (0 to 127, 128 to 255, ...) at most 8 rows name the same one
- gate_weights: float32 [65536, 2], P(('expert', 'fsdp')), may hold values from 0.25 to 1
- cotangent: bfloat16 [65536, 512], P(('expert', 'fsdp')), may hold values from -6 to 6
- weight_in: bfloat16 [512, 64, 1024], P('fsdp', 'expert'), may hold values from -0.25 to 0.25
- weight_out: bfloat16 [1024, 64, 512], P('fsdp', 'expert'), may hold values from -0.1875 to 0.1875
Outputs:
- defect: bfloat16 [65536, 512], P(('expert', 'fsdp'))
- grad_states: bfloat16 [65536, 512], P(('expert', 'fsdp'))
- grad_in: bfloat16 [512, 64, 1024], P('fsdp', 'expert')
- grad_out: bfloat16 [1024, 64, 512], P('fsdp', 'expert')
The draws below stay inside these ranges and needn't reach their ends.
Inputs may be any that keep to these rules, and one draw needn't show every extreme that they name: `expert_ids`: A knot's two ids differ. Within each aligned block of 128 knots (the knots of one device) no expert is named by more than 8 of the block's entries, a bound that some block reaches.
All inputs are finite; a program needn't handle non-finite values.
Results may differ from the reference program's by a relative error of at most 0.019.
Values may be sent and summed in bfloat16 or wider, within the bound.
No kernel may reach another device: no remote copies, remote signals or barrier semaphores. Data moves between devices by JAX's collectives and lax.ppermute only.
A program may use at most 64 MiB of HBM per device.

```python
import math
import jax
import jax.numpy as jnp
import numpy as np
from jax import lax

D = 512
H = 1024
TOK_DEV = 128
EXPERTS = 64
TOKENS = 65536
CAP = 8
N_EXPERT = 32
N_FSDP = 16


def levels(own_key, shape, pieces, low, top_value):
    def one(axis_at, shards_of):
        draws = jax.random.uniform(jax.random.fold_in(jax.random.fold_in(own_key, 6), axis_at), (shards_of,), jnp.float32, low / len(pieces), top_value / len(pieces))
        return jnp.repeat(jnp.exp(draws), shape[axis_at] // shards_of).reshape((-1,) + (1,) * (len(shape) - axis_at - 1))

    loudness = one(*pieces[0])
    for cut in pieces[1:]:
        loudness = loudness * one(*cut)
    return loudness


def shared_out(stream_key, own, number, rows, count, top, most, skew):
    order = jax.random.permutation(stream_key, count)
    packed, common = load_shares(count, rows * top, most, skew, True), load_shares(count, rows * top, most, skew, False)
    places = jnp.arange(count)

    def named(sizes, offset_by):
        used = int((sizes > 0).sum())
        fixed = max(1, used // 4)
        moved = fixed + (places - fixed + offset_by * (used - fixed)) % max(1, count - fixed)
        return jnp.zeros((count,), jnp.int32).at[order[jnp.where(places < fixed, places, moved)]].set(jnp.asarray(sizes, jnp.int32))

    sizes = jnp.where(number % 4 == 0, named(packed, number // 4), named(common, number - number // 4 - 1))
    mixed = jax.random.permutation(jax.random.fold_in(own, 3), count)
    source_of, receiver = mixed[0:count // 2 * 2:2], mixed[1:count // 2 * 2:2]
    margin = jnp.minimum(sizes[source_of] - 1, most - sizes[receiver]) // 2
    margin = jnp.where((source_of == order[0]) | (receiver == order[0]) | (sizes[receiver] == 0), 0, jnp.maximum(margin, 0))
    moved = jax.random.randint(jax.random.fold_in(own, 4), (count // 2,), 0, 1 << 20) % (margin + 1)
    sizes = sizes.at[source_of].add(-moved).at[receiver].add(moved)
    members = jnp.searchsorted(jnp.cumsum(sizes), jnp.arange(rows * top), side="right").astype(jnp.int32)
    table = members.reshape(top, rows).T
    table = table[jax.random.permutation(jax.random.fold_in(own, 1), rows)]
    offset_by = jax.random.randint(jax.random.fold_in(own, 2), (rows, 1), 0, top)
    return jnp.take_along_axis(table, (jnp.arange(top)[None, :] + offset_by) % top, axis=1)


def load_shares(number_of, total, bound, skew, full):
    portions = [(1 << 20) // math.isqrt(grade ** skew) + 1 for grade in range(1, number_of + 1)]
    largest = bound if full else min(bound, max(-(-total // number_of), total * portions[0] // sum(portions)))
    least = 1 if total - largest >= number_of - 1 else 0
    given, surplus = [largest] + [least] * (number_of - 1), total - largest - least * (number_of - 1)
    while surplus > 0:
        free = [i for i in range(1, number_of) if given[i] < largest] or [i for i in range(1, number_of) if given[i] < bound]
        mass, remaining = sum([portions[i] for i in free]), surplus
        for i in free:
            more = min(bound - given[i], max(1, remaining * portions[i] // mass), surplus)
            given[i] = given[i] + more
            surplus = surplus - more
    return np.array(given)


def centred(stream_key, extent, scale, reach, cuts=(), kind=jnp.bfloat16):
    values = jax.random.normal(stream_key, extent, jnp.float32) * scale
    if len(cuts) > 0:
        values = levels(stream_key, extent, cuts, -0.22, 0.18) * values
    return jnp.clip(values, min=-reach, max=reach).astype(kind)


def setup_inputs(seed: int = 0) -> dict:
    key_of = jax.random.split(jax.random.key(seed), 8)
    states = centred(key_of[0], (TOKENS, D), 1.0, 6.0, ((0, 512),))
    rates = centred(key_of[1], (TOKENS, D), 1.0, 6.0, ((0, 512),))
    expert_ids_keys = jax.random.split(jax.random.fold_in(key_of[2], 1), TOKENS // TOK_DEV)
    expert_ids_turns = jax.random.permutation(jax.random.fold_in(key_of[2], 3), TOKENS // TOK_DEV)
    expert_ids = jax.vmap(lambda own, number: shared_out(jax.random.fold_in(key_of[2], 2), own, number, TOK_DEV, EXPERTS, 2, CAP, 1))(expert_ids_keys, expert_ids_turns).reshape((TOKENS, 2))
    gate_weights = jnp.clip(0.25 + 0.75 * jax.random.uniform(key_of[3], (TOKENS, 2), jnp.float32) ** levels(key_of[3], (TOKENS, 2), ((0, 512),), -0.2, 0.2), 0.25, 1.0)
    cotangent = centred(key_of[4], (TOKENS, D), 1.0, 6.0, ((0, 512),))
    weight_in = centred(key_of[5], (D, EXPERTS, H), D ** -0.5, 0.25, ((0, 16), (1, 32)))
    weight_out = centred(key_of[6], (H, EXPERTS, D), H ** -0.5, 0.1875, ((0, 16), (1, 32)))
    return dict(states=states, rates=rates, expert_ids=expert_ids, gate_weights=gate_weights, cotangent=cotangent, weight_in=weight_in, weight_out=weight_out)


def activate(value):
    return value * jax.nn.sigmoid(value)


def activate_slope(value):
    sigma = jax.nn.sigmoid(value)
    return sigma * (1.0 + value * (1.0 - sigma))


def reference(states, rates, expert_ids, gate_weights, cotangent, weight_in, weight_out):
    blocks = N_EXPERT * N_FSDP
    assigned = 2 * TOK_DEV
    all_assigned = 2 * TOKENS
    ids_blocks = expert_ids.reshape(blocks, assigned)
    onehot = (ids_blocks[:, :, None] == jnp.arange(EXPERTS, dtype=jnp.int32)[None, None, :]).astype(jnp.int32)
    before = jnp.cumsum(onehot, axis=1) - onehot
    slot_index = jnp.sum(before * onehot, axis=2)
    column = (jnp.arange(blocks, dtype=jnp.int32)[:, None] * CAP + slot_index).reshape(all_assigned).astype(jnp.int32)
    flat_ids = expert_ids.reshape(all_assigned)
    slot_table = jnp.full((EXPERTS, blocks * CAP), all_assigned, jnp.int32)
    slot_table = slot_table.at[flat_ids, column].set(jnp.arange(all_assigned, dtype=jnp.int32))
    zero_row = jnp.zeros((1, D), jnp.bfloat16)
    padded_states = jnp.concatenate([states, zero_row], axis=0)
    descent = (-gate_weights[:, :, None] * cotangent[:, None, :].astype(jnp.float32)).astype(jnp.bfloat16)
    padded_descent = jnp.concatenate([descent.reshape(all_assigned, D), zero_row], axis=0)

    def per_expert(running, inputs):
        entries, expert_in, expert_out = inputs
        knot_rows = padded_states[entries // 2]
        grad_rows = padded_descent[entries]
        preact = jnp.dot(knot_rows, expert_in, preferred_element_type=jnp.float32)
        hidden = activate(preact).astype(jnp.bfloat16)
        values = jnp.dot(hidden, expert_out, preferred_element_type=jnp.float32).astype(jnp.bfloat16)
        slope = jnp.dot(grad_rows, expert_out.T, preferred_element_type=jnp.float32)
        inner = (slope * activate_slope(preact)).astype(jnp.bfloat16)
        returned = jnp.dot(inner, expert_in.T, preferred_element_type=jnp.float32).astype(jnp.bfloat16)
        grouped = (N_EXPERT, N_FSDP, CAP)
        part_in = jnp.einsum("afcd,afch->fdh", knot_rows.reshape(grouped + (D,)).astype(jnp.float32),
                             inner.reshape(grouped + (H,)).astype(jnp.float32))
        part_out = jnp.einsum("afch,afcd->fhd", hidden.reshape(grouped + (H,)).astype(jnp.float32),
                              grad_rows.reshape(grouped + (D,)).astype(jnp.float32))
        part_in = lax.optimization_barrier(part_in.astype(jnp.bfloat16))
        part_out = lax.optimization_barrier(part_out.astype(jnp.bfloat16))
        summed_in = jnp.sum(part_in.astype(jnp.float32), axis=0).astype(jnp.bfloat16)
        summed_out = jnp.sum(part_out.astype(jnp.float32), axis=0).astype(jnp.bfloat16)
        return running, (values, returned, summed_in, summed_out)

    inputs_all = (slot_table, jnp.transpose(weight_in, (1, 0, 2)), jnp.transpose(weight_out, (1, 0, 2)))
    unused, (values_all, returned_all, grad_in_all, grad_out_all) = lax.scan(
        per_expert, jnp.zeros((), jnp.float32), inputs_all)
    values_knot = values_all[flat_ids, column].reshape(TOKENS, 2, D).astype(jnp.float32)
    combined = jnp.sum(gate_weights[:, :, None] * values_knot, axis=1)
    defect = (rates.astype(jnp.float32) - combined).astype(jnp.bfloat16)
    returned_knot = returned_all[flat_ids, column].reshape(TOKENS, 2, D).astype(jnp.float32)
    grad_states = jnp.sum(returned_knot, axis=1).astype(jnp.bfloat16)
    grad_in = jnp.transpose(grad_in_all, (1, 0, 2))
    grad_out = jnp.transpose(grad_out_all, (1, 0, 2))
    return (defect, grad_states, grad_in, grad_out)
```

```python
import jax
import jax.numpy as jnp
from jax import lax
from jax.sharding import PartitionSpec as P


def activate(value):
    return value * jax.nn.sigmoid(value)


def activate_slope(value):
    sigma = jax.nn.sigmoid(value)
    return sigma * (1.0 + value * (1.0 - sigma))


def grid_of(count):
    cols = 1
    for c in range(1, count + 1):
        if count % c == 0 and c * c <= count:
            cols = c
    return count // cols, cols


def shift_pairs(count, rows, cols, step, along_cols):
    pairs = []
    for f in range(count):
        r, c = divmod(f, cols)
        if along_cols:
            g = r * cols + (c + step) % cols
        else:
            g = ((r + step) % rows) * cols + c
        pairs.append((f, g))
    return pairs


def ring_gather(piece, rows, cols):
    count = rows * cols
    f = lax.axis_index("fsdp")
    r, c = f // cols, f % cols
    got = [piece] + [
        lax.ppermute(piece, "fsdp", shift_pairs(count, rows, cols, s, True)) for s in range(1, cols)
    ]
    rev = jnp.stack([got[(-k) % cols] for k in range(cols)])
    row = jnp.roll(rev, c, axis=0)
    got = [row] + [
        lax.ppermute(row, "fsdp", shift_pairs(count, rows, cols, s, False)) for s in range(1, rows)
    ]
    rev = jnp.stack([got[(-k) % rows] for k in range(rows)])
    whole = jnp.roll(rev, r, axis=0)
    return whole.reshape(count, piece.shape[0])


def ring_reduce_scatter(chunks, rows, cols):
    count = rows * cols
    f = lax.axis_index("fsdp")
    r, c = f // cols, f % cols
    grid = chunks.reshape(rows, cols, chunks.shape[1])
    total = lax.dynamic_index_in_dim(grid, r, 0, keepdims=False).astype(jnp.float32)
    for s in range(1, rows):
        part = lax.dynamic_index_in_dim(grid, (r + s) % rows, 0, keepdims=False)
        total = total + lax.ppermute(part, "fsdp", shift_pairs(count, rows, cols, s, False)).astype(
            jnp.float32
        )
    mine = lax.dynamic_index_in_dim(total, c, 0, keepdims=False)
    for s in range(1, cols):
        part = lax.dynamic_index_in_dim(total, (c + s) % cols, 0, keepdims=False)
        mine = mine + lax.ppermute(part, "fsdp", shift_pairs(count, rows, cols, s, True))
    return mine


def on_device(states, rates, expert_ids, gate_weights, cotangent, weight_in, weight_out):
    row_count = states.shape[0]
    feature = states.shape[1]
    local_count = weight_in.shape[1]
    hidden_width = weight_in.shape[2]
    groups = lax.axis_size("expert")
    fsdp_count = lax.axis_size("fsdp")
    rows, cols = grid_of(fsdp_count)
    experts_all = local_count * groups
    capacity = max(2, 4 * row_count // experts_all)
    assigned = 2 * row_count

    in_size = weight_in.size
    pieces = jnp.concatenate([weight_in.reshape(-1), weight_out.reshape(-1)])
    gathered = ring_gather(pieces, rows, cols)
    full_in = gathered[:, :in_size].reshape((fsdp_count * weight_in.shape[0],) + weight_in.shape[1:])
    full_out = gathered[:, in_size:].reshape((fsdp_count * weight_out.shape[0],) + weight_out.shape[1:])

    flat_ids = expert_ids.reshape(assigned)
    onehot = (flat_ids[:, None] == jnp.arange(experts_all, dtype=jnp.int32)[None, :]).astype(
        jnp.int32
    )
    before = jnp.cumsum(onehot, axis=0) - onehot
    slot_index = jnp.sum(before * onehot, axis=1)
    position = flat_ids * capacity + slot_index
    source = jnp.full((experts_all * capacity,), assigned, jnp.int32)
    source = source.at[position].set(jnp.arange(assigned, dtype=jnp.int32))
    zero_row = jnp.zeros((1, feature), jnp.bfloat16)
    padded_states = jnp.concatenate([states, zero_row], axis=0)
    descent = (-gate_weights[:, :, None] * cotangent[:, None, :].astype(jnp.float32)).astype(
        jnp.bfloat16
    )
    padded_descent = jnp.concatenate([descent.reshape(assigned, feature), zero_row], axis=0)
    send_shape = (experts_all, capacity, feature)
    send_knots = padded_states[source // 2].reshape(send_shape)
    send_grads = padded_descent[source].reshape(send_shape)
    send = jnp.concatenate([send_knots, send_grads], axis=1)
    got = lax.all_to_all(send, "expert", split_axis=0, concat_axis=0, tiled=True)
    got = got.reshape(groups, local_count, 2 * capacity, feature)
    knot_rows = got[:, :, :capacity]
    grad_rows = got[:, :, capacity:]

    preact = jnp.einsum("secd,deh->sech", knot_rows, full_in, preferred_element_type=jnp.float32)
    hidden = activate(preact).astype(jnp.bfloat16)
    values = jnp.einsum("sech,hed->secd", hidden, full_out, preferred_element_type=jnp.float32)
    slope = jnp.einsum("secd,hed->sech", grad_rows, full_out, preferred_element_type=jnp.float32)
    inner = (slope * activate_slope(preact)).astype(jnp.bfloat16)

    part_in = jnp.einsum(
        "secd,sech->deh", knot_rows, inner, preferred_element_type=jnp.float32
    ).astype(jnp.bfloat16)
    part_out = jnp.einsum(
        "sech,secd->hed", hidden, grad_rows, preferred_element_type=jnp.float32
    ).astype(jnp.bfloat16)
    chunks = jnp.concatenate(
        [part_in.reshape(fsdp_count, -1), part_out.reshape(fsdp_count, -1)], axis=1
    )
    summed = ring_reduce_scatter(chunks, rows, cols).astype(jnp.bfloat16)
    grad_in = summed[:in_size].reshape(weight_in.shape)
    grad_out = summed[in_size:].reshape(weight_out.shape)

    returned = jnp.einsum("sech,deh->secd", inner, full_in, preferred_element_type=jnp.float32)
    back = jnp.concatenate(
        [values.astype(jnp.bfloat16), returned.astype(jnp.bfloat16)], axis=2
    ).reshape(experts_all, 2 * capacity, feature)
    back = lax.all_to_all(back, "expert", split_axis=0, concat_axis=0, tiled=True)
    back = back.reshape(experts_all * capacity * 2, feature)
    values_knot = back[(position // capacity) * (2 * capacity) + position % capacity]
    values_knot = values_knot.reshape(row_count, 2, feature).astype(jnp.float32)
    combined = jnp.sum(gate_weights[:, :, None] * values_knot, axis=1)
    defect = (rates.astype(jnp.float32) - combined).astype(jnp.bfloat16)
    returned_knot = back[(position // capacity) * (2 * capacity) + capacity + position % capacity]
    returned_knot = returned_knot.reshape(row_count, 2, feature).astype(jnp.float32)
    grad_states = jnp.sum(returned_knot, axis=1).astype(jnp.bfloat16)
    return (defect, grad_states, grad_in, grad_out)


def solution(mesh):
    placed = (
        P(("expert", "fsdp"), None),
        P(("expert", "fsdp"), None),
        P(("expert", "fsdp"), None),
        P(("expert", "fsdp"), None),
        P(("expert", "fsdp"), None),
        P("fsdp", "expert", None),
        P("fsdp", "expert", None),
    )
    return jax.shard_map(
        on_device,
        mesh=mesh,
        in_specs=placed,
        out_specs=(
            P(("expert", "fsdp"), None),
            P(("expert", "fsdp"), None),
            P("fsdp", "expert", None),
            P("fsdp", "expert", None),
        ),
        check_vma=False,
    )
```

```python
import jax
import jax.numpy as jnp
from jax import lax
from jax.sharding import PartitionSpec as P


def activate(value):
    return value * jax.nn.sigmoid(value)


def activate_slope(value):
    sigma = jax.nn.sigmoid(value)
    return sigma * (1.0 + value * (1.0 - sigma))


def grid_of(count):
    cols = 1
    for c in range(1, count + 1):
        if count % c == 0 and c * c <= count:
            cols = c
    return count // cols, cols


def shift_pairs(count, rows, cols, step, along_cols):
    pairs = []
    for f in range(count):
        r, c = divmod(f, cols)
        if along_cols:
            g = r * cols + (c + step) % cols
        else:
            g = ((r + step) % rows) * cols + c
        pairs.append((f, g))
    return pairs


def pick(pieces, index):
    count = len(pieces)
    out = []
    for i in range(count):
        chosen = pieces[count - 1]
        for k in range(count - 2, -1, -1):
            chosen = jnp.where((index - k) % count == i, pieces[k], chosen)
        out.append(chosen)
    return jnp.stack(out)


def axis_gather(piece, rows, cols, along_cols):
    count = rows * cols
    f = lax.axis_index("fsdp")
    size, index = (cols, f % cols) if along_cols else (rows, f // cols)
    got = [piece] + [
        lax.ppermute(piece, "fsdp", shift_pairs(count, rows, cols, s, along_cols)) for s in range(1, size)
    ]
    return pick(got, index)


def grid_gather(piece, rows, cols, cols_first):
    if cols_first:
        line = axis_gather(piece, rows, cols, True)
        return axis_gather(line, rows, cols, False)
    line = axis_gather(piece, rows, cols, False)
    return jnp.swapaxes(axis_gather(line, rows, cols, True), 0, 1)


def grid_reduce_scatter(parts, rows, cols, rows_first):
    count = rows * cols
    f = lax.axis_index("fsdp")
    r, c = f // cols, f % cols
    if rows_first:
        total = lax.dynamic_index_in_dim(parts, r, 0, keepdims=False).astype(jnp.float32)
        for s in range(1, rows):
            part = lax.dynamic_index_in_dim(parts, (r + s) % rows, 0, keepdims=False)
            got = lax.ppermute(part, "fsdp", shift_pairs(count, rows, cols, s, False))
            total = total + got.astype(jnp.float32)
        mine = lax.dynamic_index_in_dim(total, c, 0, keepdims=False)
        for s in range(1, cols):
            part = lax.dynamic_index_in_dim(total, (c + s) % cols, 0, keepdims=False)
            mine = mine + lax.ppermute(part, "fsdp", shift_pairs(count, rows, cols, s, True))
        return mine
    total = lax.dynamic_index_in_dim(parts, c, 1, keepdims=False).astype(jnp.float32)
    for s in range(1, cols):
        part = lax.dynamic_index_in_dim(parts, (c + s) % cols, 1, keepdims=False)
        got = lax.ppermute(part, "fsdp", shift_pairs(count, rows, cols, s, True))
        total = total + got.astype(jnp.float32)
    mine = lax.dynamic_index_in_dim(total, r, 0, keepdims=False)
    for s in range(1, rows):
        part = lax.dynamic_index_in_dim(total, (r + s) % rows, 0, keepdims=False)
        mine = mine + lax.ppermute(part, "fsdp", shift_pairs(count, rows, cols, s, False))
    return mine


def on_device(states, rates, expert_ids, gate_weights, cotangent, weight_in, weight_out):
    row_count = states.shape[0]
    feature = states.shape[1]
    local_count = weight_in.shape[1]
    hidden_width = weight_in.shape[2]
    groups = lax.axis_size("expert")
    fsdp_count = lax.axis_size("fsdp")
    rows, cols = grid_of(fsdp_count)
    experts_all = local_count * groups
    capacity = max(2, 4 * row_count // experts_all)
    assigned = 2 * row_count

    shard_in, shard_out = weight_in.shape[0], weight_out.shape[0]
    full_in = grid_gather(weight_in, rows, cols, True).reshape(
        (fsdp_count * shard_in,) + weight_in.shape[1:]
    )
    full_out = grid_gather(weight_out, rows, cols, False).reshape(
        (fsdp_count * shard_out,) + weight_out.shape[1:]
    )

    flat_ids = expert_ids.reshape(assigned)
    onehot = (flat_ids[:, None] == jnp.arange(experts_all, dtype=jnp.int32)[None, :]).astype(
        jnp.int32
    )
    before = jnp.cumsum(onehot, axis=0) - onehot
    slot_index = jnp.sum(before * onehot, axis=1)
    position = flat_ids * capacity + slot_index
    source = jnp.full((experts_all * capacity,), assigned, jnp.int32)
    source = source.at[position].set(jnp.arange(assigned, dtype=jnp.int32))
    zero_row = jnp.zeros((1, feature), jnp.bfloat16)
    padded_states = jnp.concatenate([states, zero_row], axis=0)
    descent = (-gate_weights[:, :, None] * cotangent[:, None, :].astype(jnp.float32)).astype(
        jnp.bfloat16
    )
    padded_descent = jnp.concatenate([descent.reshape(assigned, feature), zero_row], axis=0)
    send_shape = (experts_all, capacity, feature)
    send_knots = padded_states[source // 2].reshape(send_shape)
    send_grads = padded_descent[source].reshape(send_shape)
    send = jnp.concatenate([send_knots, send_grads], axis=1)
    got = lax.all_to_all(send, "expert", split_axis=0, concat_axis=0, tiled=True)
    got = got.reshape(groups, local_count, 2 * capacity, feature)
    knot_rows = got[:, :, :capacity]
    grad_rows = got[:, :, capacity:]

    preact = jnp.einsum("secd,deh->sech", knot_rows, full_in, preferred_element_type=jnp.float32)
    hidden = activate(preact).astype(jnp.bfloat16)
    values = jnp.einsum("sech,hed->secd", hidden, full_out, preferred_element_type=jnp.float32)
    slope = jnp.einsum("secd,hed->sech", grad_rows, full_out, preferred_element_type=jnp.float32)
    inner = (slope * activate_slope(preact)).astype(jnp.bfloat16)

    part_in = jnp.einsum(
        "secd,sech->deh", knot_rows, inner, preferred_element_type=jnp.float32
    ).astype(jnp.bfloat16)
    part_out = jnp.einsum(
        "sech,secd->hed", hidden, grad_rows, preferred_element_type=jnp.float32
    ).astype(jnp.bfloat16)
    grad_in = grid_reduce_scatter(
        part_in.reshape((rows, cols, shard_in) + weight_in.shape[1:]), rows, cols, True
    ).astype(jnp.bfloat16)
    grad_out = grid_reduce_scatter(
        part_out.reshape((rows, cols, shard_out) + weight_out.shape[1:]), rows, cols, False
    ).astype(jnp.bfloat16)

    returned = jnp.einsum("sech,deh->secd", inner, full_in, preferred_element_type=jnp.float32)
    back = jnp.concatenate(
        [values.astype(jnp.bfloat16), returned.astype(jnp.bfloat16)], axis=2
    ).reshape(experts_all, 2 * capacity, feature)
    back = lax.all_to_all(back, "expert", split_axis=0, concat_axis=0, tiled=True)
    back = back.reshape(experts_all * capacity * 2, feature)
    values_knot = back[(position // capacity) * (2 * capacity) + position % capacity]
    values_knot = values_knot.reshape(row_count, 2, feature).astype(jnp.float32)
    combined = jnp.sum(gate_weights[:, :, None] * values_knot, axis=1)
    defect = (rates.astype(jnp.float32) - combined).astype(jnp.bfloat16)
    returned_knot = back[(position // capacity) * (2 * capacity) + capacity + position % capacity]
    returned_knot = returned_knot.reshape(row_count, 2, feature).astype(jnp.float32)
    grad_states = jnp.sum(returned_knot, axis=1).astype(jnp.bfloat16)
    return (defect, grad_states, grad_in, grad_out)


def solution(mesh):
    placed = (
        P(("expert", "fsdp"), None),
        P(("expert", "fsdp"), None),
        P(("expert", "fsdp"), None),
        P(("expert", "fsdp"), None),
        P(("expert", "fsdp"), None),
        P("fsdp", "expert", None),
        P("fsdp", "expert", None),
    )
    return jax.shard_map(
        on_device,
        mesh=mesh,
        in_specs=placed,
        out_specs=(
            P(("expert", "fsdp"), None),
            P(("expert", "fsdp"), None),
            P("fsdp", "expert", None),
            P("fsdp", "expert", None),
        ),
        check_vma=False,
    )
```

```python
import jax
import jax.numpy as jnp
from jax import lax
from jax.sharding import PartitionSpec as P


def activate(value):
    return value * jax.nn.sigmoid(value)


def activate_slope(value):
    sigma = jax.nn.sigmoid(value)
    return sigma * (1.0 + value * (1.0 - sigma))


def grid_of(count):
    cols = 1
    for c in range(1, count + 1):
        if count % c == 0 and c * c <= count:
            cols = c
    return count // cols, cols


def shift_pairs(count, rows, cols, step, along_cols):
    pairs = []
    for f in range(count):
        r, c = divmod(f, cols)
        if along_cols:
            g = r * cols + (c + step) % cols
        else:
            g = ((r + step) % rows) * cols + c
        pairs.append((f, g))
    return pairs


def pick(pieces, index):
    count = len(pieces)
    out = []
    for i in range(count):
        chosen = pieces[count - 1]
        for k in range(count - 2, -1, -1):
            chosen = jnp.where((index - k) % count == i, pieces[k], chosen)
        out.append(chosen)
    return jnp.stack(out)


def axis_gather(piece, rows, cols, along_cols):
    count = rows * cols
    f = lax.axis_index("fsdp")
    size, index = (cols, f % cols) if along_cols else (rows, f // cols)
    got = [piece] + [
        lax.ppermute(piece, "fsdp", shift_pairs(count, rows, cols, s, along_cols)) for s in range(1, size)
    ]
    return pick(got, index)


def grid_gather(piece, rows, cols, cols_first):
    if cols_first:
        line = axis_gather(piece, rows, cols, True)
        return axis_gather(line, rows, cols, False)
    line = axis_gather(piece, rows, cols, False)
    return jnp.swapaxes(axis_gather(line, rows, cols, True), 0, 1)


def grid_reduce_scatter(parts, rows, cols, rows_first):
    count = rows * cols
    f = lax.axis_index("fsdp")
    r, c = f // cols, f % cols
    if rows_first:
        total = lax.dynamic_index_in_dim(parts, r, 0, keepdims=False).astype(jnp.float32)
        for s in range(1, rows):
            part = lax.dynamic_index_in_dim(parts, (r + s) % rows, 0, keepdims=False)
            got = lax.ppermute(part, "fsdp", shift_pairs(count, rows, cols, s, False))
            total = total + got.astype(jnp.float32)
        mine = lax.dynamic_index_in_dim(total, c, 0, keepdims=False)
        for s in range(1, cols):
            part = lax.dynamic_index_in_dim(total, (c + s) % cols, 0, keepdims=False)
            mine = mine + lax.ppermute(part, "fsdp", shift_pairs(count, rows, cols, s, True))
        return mine
    total = lax.dynamic_index_in_dim(parts, c, 1, keepdims=False).astype(jnp.float32)
    for s in range(1, cols):
        part = lax.dynamic_index_in_dim(parts, (c + s) % cols, 1, keepdims=False)
        got = lax.ppermute(part, "fsdp", shift_pairs(count, rows, cols, s, True))
        total = total + got.astype(jnp.float32)
    mine = lax.dynamic_index_in_dim(total, r, 0, keepdims=False)
    for s in range(1, rows):
        part = lax.dynamic_index_in_dim(total, (r + s) % rows, 0, keepdims=False)
        mine = mine + lax.ppermute(part, "fsdp", shift_pairs(count, rows, cols, s, False))
    return mine


def body(states, rates, expert_ids, gate_weights, cotangent, weight_in, weight_out):
    row_count = states.shape[0]
    feature = states.shape[1]
    local_count = weight_in.shape[1]
    groups = lax.axis_size("expert")
    fsdp_count = lax.axis_size("fsdp")
    rows, cols = grid_of(fsdp_count)
    experts_all = local_count * groups
    capacity = max(2, 4 * row_count // experts_all)
    assigned = 2 * row_count

    shard_in, shard_out = weight_in.shape[0], weight_out.shape[0]
    flat_ids = expert_ids.reshape(assigned)
    onehot = (flat_ids[:, None] == jnp.arange(experts_all, dtype=jnp.int32)[None, :]).astype(
        jnp.int32
    )
    before = jnp.cumsum(onehot, axis=0) - onehot
    slot_index = jnp.sum(before * onehot, axis=1)
    position = flat_ids * capacity + slot_index
    source = jnp.full((experts_all * capacity,), assigned, jnp.int32)
    source = source.at[position].set(jnp.arange(assigned, dtype=jnp.int32))
    zero_row = jnp.zeros((1, feature), jnp.bfloat16)
    padded_states = jnp.concatenate([states, zero_row], axis=0)
    descent = (-gate_weights[:, :, None] * cotangent[:, None, :].astype(jnp.float32)).astype(
        jnp.bfloat16
    )
    padded_descent = jnp.concatenate([descent.reshape(assigned, feature), zero_row], axis=0)
    send_shape = (experts_all, capacity, feature)
    send_knots = padded_states[source // 2].reshape(send_shape)
    send_grads = padded_descent[source].reshape(send_shape)
    send = jnp.concatenate([send_knots, send_grads], axis=1)
    got = lax.all_to_all(send, "expert", split_axis=0, concat_axis=0, tiled=True)
    full_in = lax.all_gather(weight_in, "fsdp", axis=0, tiled=True)
    full_out = grid_gather(weight_out, rows, cols, False).reshape(
        (fsdp_count * shard_out,) + weight_out.shape[1:]
    )
    got = got.reshape(groups, local_count, 2 * capacity, feature)
    knot_rows = got[:, :, :capacity]
    grad_rows = got[:, :, capacity:]

    preact = jnp.einsum("secd,deh->sech", knot_rows, full_in, preferred_element_type=jnp.float32)
    hidden = activate(preact).astype(jnp.bfloat16)
    part_out = jnp.einsum(
        "sech,secd->hed", hidden, grad_rows, preferred_element_type=jnp.float32
    ).astype(jnp.bfloat16)
    grad_out = grid_reduce_scatter(
        part_out.reshape((rows, cols, shard_out) + weight_out.shape[1:]), rows, cols, False
    ).astype(jnp.bfloat16)
    values = jnp.einsum("sech,hed->secd", hidden, full_out, preferred_element_type=jnp.float32)
    slope = jnp.einsum("secd,hed->sech", grad_rows, full_out, preferred_element_type=jnp.float32)
    inner = (slope * activate_slope(preact)).astype(jnp.bfloat16)
    returned = jnp.einsum("sech,deh->secd", inner, full_in, preferred_element_type=jnp.float32)
    back = jnp.concatenate(
        [values.astype(jnp.bfloat16), returned.astype(jnp.bfloat16)], axis=2
    ).reshape(experts_all, 2 * capacity, feature)
    back = lax.all_to_all(back, "expert", split_axis=0, concat_axis=0, tiled=True)
    part_in = jnp.einsum(
        "secd,sech->deh", knot_rows, inner, preferred_element_type=jnp.float32
    ).astype(jnp.bfloat16)
    grad_in = grid_reduce_scatter(
        part_in.reshape((rows, cols, shard_in) + weight_in.shape[1:]), rows, cols, True
    ).astype(jnp.bfloat16)
    back = back.reshape(experts_all * capacity * 2, feature)
    values_knot = back[(position // capacity) * (2 * capacity) + position % capacity]
    values_knot = values_knot.reshape(row_count, 2, feature).astype(jnp.float32)
    combined = jnp.sum(gate_weights[:, :, None] * values_knot, axis=1)
    defect = (rates.astype(jnp.float32) - combined).astype(jnp.bfloat16)
    returned_knot = back[(position // capacity) * (2 * capacity) + capacity + position % capacity]
    returned_knot = returned_knot.reshape(row_count, 2, feature).astype(jnp.float32)
    grad_states = jnp.sum(returned_knot, axis=1).astype(jnp.bfloat16)
    return (defect, grad_states, grad_in, grad_out)


def solution(mesh):
    placed = (
        P(("expert", "fsdp"), None),
        P(("expert", "fsdp"), None),
        P(("expert", "fsdp"), None),
        P(("expert", "fsdp"), None),
        P(("expert", "fsdp"), None),
        P("fsdp", "expert", None),
        P("fsdp", "expert", None),
    )
    return jax.shard_map(
        body,
        mesh=mesh,
        in_specs=placed,
        out_specs=(
            P(("expert", "fsdp"), None),
            P(("expert", "fsdp"), None),
            P("fsdp", "expert", None),
            P("fsdp", "expert", None),
        ),
        check_vma=False,
    )
```
